32 devices in a mesh: batch: 4 (over x, core), cache: 8 (over z, y).
Axes of the slice: x: 2, y: 2, z: 4, core: 2. Of those that a mesh axis runs over, the one named last changes fastest.
Arguments:
- arrivals: bfloat16 [16, 4, 4096], P('batch', None, 'cache'), may hold values from -6 to 6
- norm_gain: float32 [4096], replicated, may hold values from 0.25 to 1.75
- qkv_weight: bfloat16 [4096, 6144], P(None, 'cache'), may hold values from -0.09375 to 0.09375
- out_weight: bfloat16 [4096, 4096], P('cache'), may hold values from -0.09375 to 0.09375
- kv_cache: bfloat16 [16, 16, 2, 8, 128, 128], P('batch', 'cache'), as said below
- slot: int32 [16], replicated, may hold values from 0 to 15, each once
- positions: int32 [16], P('batch'), may hold values from 1664 to 2044
- tile_lists: int32 [16, 8], P('batch'), may hold values from 0 to 15, as said below
Outputs:
- attended: bfloat16 [16, 4, 4096], P('batch', None, 'cache')
The draws below stay inside these ranges and needn't reach their ends.
Inputs may be any that keep to these rules, and one draw needn't show every extreme that they name: `tile_lists`: tiles of a row are distinct; the first is the tile of position positions - 1, the others lie at most 12 tiles before it. `kv_cache`: entries are of magnitude at most 240.
All inputs are finite; a program needn't handle non-finite values.
Results may differ from the reference program's by a relative error of at most 0.022.
Values may be sent and summed in bfloat16 or wider, within the bound.
A program may use at most 64 MiB of HBM per device.

```python
import math
import jax
import jax.numpy as jnp
from jax import lax

D = 4096
HEADS = 32
KVH = 8
HD = 128
TILE = 128
STEPS = 4
WIN = 8
NEAR = 12
IMW = 64
CW = 16
REQS = 16
TILES = 16


def request_plan(key):
    first_key, second_key = jax.random.split(jax.random.fold_in(key, 7))
    lowest = (NEAR + 1) * TILE
    highest = TILES * TILE - STEPS
    position = jax.random.randint(first_key, (REQS,), lowest, highest + 1, dtype=jnp.int32)
    position = position.at[0].set(highest).at[1].set(lowest)
    current = (position - 1) // TILE
    row_keys = jax.random.split(second_key, REQS)
    shuffled = jax.vmap(lambda row_key: jax.random.permutation(row_key, NEAR))(row_keys)[:, :WIN - 1].astype(jnp.int32)
    farthest = (NEAR - 1 - jnp.arange(WIN - 1, dtype=jnp.int32)).astype(jnp.int32)
    shuffled = shuffled.at[1].set(farthest)
    listing = jnp.concatenate([current[:, None], current[:, None] - 1 - shuffled], axis=1)
    return (position.astype(jnp.int32), listing.astype(jnp.int32))


def draw_positions(key, part):
    return request_plan(key)[0]


def draw_tile_lists(key, part):
    return request_plan(key)[1]


def draw_kv_cache(key, part):
    base_key = jax.random.fold_in(jax.random.fold_in(key, 11), 0)
    values = jnp.clip(jax.random.normal(base_key, (REQS, TILES, 2, KVH, TILE, HD), jnp.float32), -6.0, 6.0)
    return values.astype(jnp.bfloat16)


def block_levels(stream_key, dims, cuts, least, largest):
    gain, own = 1.0, jax.random.fold_in(stream_key, 6)
    for dim, parts in cuts:
        draws = jnp.exp(jax.random.uniform(jax.random.fold_in(own, dim), (parts,), jnp.float32, least / len(cuts), largest / len(cuts)))
        gain = gain * jnp.repeat(draws, dims[dim] // parts).reshape([-1 if axis == dim else 1 for axis in range(len(dims))])
    return gain


def normal_values(own_key, shape, spread, limit, cuts=(), held_as=jnp.bfloat16):
    values = jax.random.normal(own_key, shape, jnp.float32) * spread
    if len(cuts) > 0:
        values = block_levels(own_key, shape, cuts, -0.22, 0.18) * values
    return jnp.clip(values, min=-limit, max=limit).astype(held_as)


def setup_inputs(seed: int = 0) -> dict:
    keys = jax.random.split(jax.random.key(seed), 9)
    return {
        "arrivals": normal_values(keys[0], (REQS, STEPS, D), 1.0, 6.0, ((0, 4), (2, 8))),
        "norm_gain": jnp.clip(1.0 + 0.15 * jax.random.normal(keys[1], (D,), jnp.float32), 0.25, 1.75),
        "qkv_weight": normal_values(keys[2], (D, KVH * (HEADS // KVH + 2) * HD), D ** -0.5, 0.09375, ((1, 8),)),
        "out_weight": normal_values(keys[3], (HEADS * HD, D), (HEADS * HD) ** -0.5, 0.09375, ((0, 8),)),
        "kv_cache": draw_kv_cache(jax.random.fold_in(keys[8], 71), 0),
        "slot": jax.random.permutation(keys[5], REQS).astype(jnp.int32),
        "positions": draw_positions(jax.random.fold_in(keys[8], 71), 0),
        "tile_lists": draw_tile_lists(jax.random.fold_in(keys[8], 71), 0),
    }


epsilon = 1e-05

def window_mask(query_pos, key_pos):
    return jnp.abs(key_pos % IMW - query_pos % IMW) <= CW

def reference(arrivals, norm_gain, qkv_weight, out_weight, kv_cache, slot, positions, tile_lists):
    groups = HEADS // KVH
    inverse = jnp.argsort(slot).astype(jnp.int32)
    ordered = jnp.take(arrivals, inverse, axis=0).astype(jnp.float32)
    normed = (ordered * lax.rsqrt(lax.optimization_barrier(jnp.mean(ordered * ordered, axis=-1, keepdims=True)) + epsilon) * norm_gain).astype(jnp.bfloat16)
    projected = jnp.dot(normed.reshape(REQS * STEPS, D), qkv_weight, preferred_element_type=jnp.float32)
    projected = projected.astype(jnp.bfloat16).reshape(REQS, STEPS, KVH, groups + 2, HD)
    score_scale = 1.0 / math.sqrt(HD)
    step_index = jnp.arange(STEPS, dtype=jnp.int32)

    def one_request(inputs):
        heads_row, cache_row, position, listing = inputs
        queries = heads_row[:, :, :groups].astype(jnp.float32)
        new_keys = heads_row[:, :, groups].astype(jnp.float32)
        new_vals = heads_row[:, :, groups + 1].astype(jnp.float32)
        chosen = jnp.take(cache_row, listing.astype(jnp.int32), axis=0).astype(jnp.float32)
        key_pos = listing[:, None] * TILE + jnp.arange(TILE, dtype=jnp.int32)[None, :]
        query_pos = position + step_index
        key_valid = (key_pos[None] < position) & window_mask(query_pos[:, None, None], key_pos[None])
        scores = jnp.einsum('sjgd,wjkd->jgswk', queries, chosen[:, 0]) * score_scale
        new_scores = jnp.einsum('sjgd,ujd->jgsu', queries, new_keys) * score_scale
        new_valid = (step_index[:, None] >= step_index[None, :]) & window_mask(query_pos[:, None], query_pos[None, :])
        top_score = jnp.maximum(lax.optimization_barrier(jnp.max(jnp.where(key_valid, scores, -jnp.inf), axis=(-2, -1))), lax.optimization_barrier(jnp.max(jnp.where(new_valid, new_scores, -jnp.inf), axis=-1)))
        weights = jnp.where(key_valid, jnp.exp(scores - top_score[..., None, None]), 0.0)
        new_weights = jnp.where(new_valid, jnp.exp(new_scores - top_score[..., None]), 0.0)
        totals = lax.optimization_barrier(jnp.sum(weights, axis=(-2, -1))) + lax.optimization_barrier(jnp.sum(new_weights, axis=-1))
        numerator = jnp.einsum('jgswk,wjkd->jgsd', weights.astype(jnp.bfloat16).astype(jnp.float32), chosen[:, 1])
        numerator = numerator + jnp.einsum('jgsu,ujd->jgsd', new_weights.astype(jnp.bfloat16).astype(jnp.float32), new_vals)
        attention = (numerator / totals[..., None]).astype(jnp.bfloat16)
        return attention.transpose(2, 0, 1, 3).reshape(STEPS, HEADS * HD)
    attention = lax.map(one_request, (projected, kv_cache, positions, tile_lists))
    attended = jnp.dot(attention.reshape(REQS * STEPS, HEADS * HD), out_weight, preferred_element_type=jnp.float32)
    return attended.astype(jnp.bfloat16).reshape(REQS, STEPS, D)
```

```python
import functools
import math

import jax
import jax.numpy as jnp
from jax import lax
from jax.experimental import pallas as pl
from jax.experimental.pallas import tpu as pltpu
from jax.sharding import PartitionSpec as P

HEADS = 32
KVH = 8
HD = 128
TILE = 128
IMW = 64
CW = 16
GROUPS = HEADS // KVH

epsilon = 1e-05
very_low = -1e30
f32 = jnp.float32
bf16 = jnp.bfloat16


def kernel(nb, n, slot, pos, lists, arr, gain, wq_hbm, wo_hbm, kv_hbm, out,
           wq, wo, kv, abuf, xrow, xg, prow, pg, pn, ps, arow, po, ro,
           wsem, ssem, rsem, bssem, brsem):
    b = lax.axis_index("batch")
    me = lax.axis_index("cache")
    rows, steps, feat = arr.shape
    depth, cols = wq_hbm.shape
    hs = wo_hbm.shape[0] // HD
    tiles = kv_hbm.shape[1]
    grp = cols // HD
    per = (GROUPS + 2) // grp
    hq = hs * steps
    toks = rows * steps
    nq = rows * hq

    loads_q = [
        pltpu.make_async_copy(wq_hbm.at[pl.ds(c * feat, feat)], wq.at[c], wsem.at[c])
        for c in range(n)
    ]
    load_kv = [
        pltpu.make_async_copy(kv_hbm.at[r], kv.at[r], wsem.at[n + r]) for r in range(rows)
    ]
    loads_o = [
        pltpu.make_async_copy(wo_hbm.at[:, pl.ds(c * feat, feat)], wo.at[c], wsem.at[n + rows + c])
        for c in range(n)
    ]
    own = pltpu.make_async_copy(arr, abuf.at[pl.ds(b * rows, rows)], wsem.at[2 * n + rows])
    own.start()
    for c in loads_q:
        c.start()

    barrier = pltpu.get_barrier_semaphore()
    for k in range(1, nb):
        pl.semaphore_signal(barrier, inc=1, device_id=(lax.rem(b + k, nb), me),
                            device_id_type=pl.DeviceIdType.MESH)
    for k in range(1, n):
        pl.semaphore_signal(barrier, inc=1, device_id=(b, lax.rem(me + k, n)),
                            device_id_type=pl.DeviceIdType.MESH)
    pl.semaphore_wait(barrier, nb + n - 2)

    def exchange(src, dst, phase, k, to):
        return pltpu.make_async_remote_copy(
            src_ref=src, dst_ref=dst, send_sem=ssem.at[phase, k], recv_sem=rsem.at[phase, k],
            device_id=(b, to), device_id_type=pl.DeviceIdType.MESH)

    def batch_copy(k, at):
        return pltpu.make_async_remote_copy(
            src_ref=arr, dst_ref=abuf.at[pl.ds(at * rows, rows)], send_sem=bssem.at[k],
            recv_sem=brsem.at[k], device_id=(lax.rem(b + k, nb), me),
            device_id_type=pl.DeviceIdType.MESH)

    for k in range(1, nb):
        batch_copy(k, b).start()
    for c in load_kv + loads_o:
        c.start()
    own.wait()
    for k in range(1, nb):
        batch_copy(k, lax.rem(b + nb - k, nb)).wait_recv()
    for r in range(rows):
        place = jnp.int32(0)
        for i in range(nb * rows):
            place = jnp.where(slot[i] == b * rows + r, i, place)
        xrow[r * steps:(r + 1) * steps, :] = abuf[place].astype(f32)
    xg[me] = xrow[...].astype(bf16)
    for k in range(1, n):
        exchange(xg.at[me], xg.at[me], 0, k, lax.rem(me + k, n)).start()
    for k in range(1, n):
        frm = lax.rem(me + n - k, n)
        exchange(xg.at[frm], xg.at[frm], 0, k, lax.rem(me + k, n)).wait_recv()

    square = jnp.zeros((toks, 1), f32)
    for c in range(n):
        x = xg[c].astype(f32)
        square = square + jnp.sum(x * x, axis=1, keepdims=True)
    scale = lax.rsqrt(square / depth + epsilon)
    acc = jnp.zeros((toks, cols), f32)
    for c in range(n):
        loads_q[c].wait()
        y = (xg[c].astype(f32) * scale * gain[:, c * feat:(c + 1) * feat]).astype(bf16)
        acc = acc + jnp.dot(y, wq[c], preferred_element_type=f32)
    for r in range(rows):
        for g in range(grp):
            prow[r, g * steps:(g + 1) * steps, :] = acc[r * steps:(r + 1) * steps,
                                                        g * HD:(g + 1) * HD]
    pg[me] = prow[...].astype(bf16)
    for k in range(1, n):
        exchange(pg.at[me], pg.at[me], 1, k, lax.rem(me + k, n)).start()

    q_rows = GROUPS * steps
    row_i = lax.broadcasted_iota(jnp.int32, (q_rows, TILE), 0)
    lane_i = lax.broadcasted_iota(jnp.int32, (q_rows, TILE), 1)
    masks = []
    for r in range(rows):
        p = pos[r]
        near = jnp.abs((lane_i & (IMW - 1)) - ((p + (row_i & (steps - 1))) & (IMW - 1))) <= CW
        per_tile = []
        for t in range(tiles):
            tile_id = me * tiles + t
            hit = jnp.int32(0)
            for w in range(lists.shape[1]):
                hit = hit + jnp.where(lists[r, w] == tile_id, 1, 0)
            limit = jnp.where(hit > 0, p - tile_id * TILE, 0)
            per_tile.append(near & (lane_i < limit))
        masks.append(per_tile)

    for k in range(1, n):
        frm = lax.rem(me + n - k, n)
        exchange(pg.at[frm], pg.at[frm], 1, k, lax.rem(me + k, n)).wait_recv()
    for c in load_kv:
        c.wait()

    score_scale = 1.0 / math.sqrt(HD)
    dests = GROUPS // hs
    my_j = me // dests

    def head_rows(j, r):
        if per == 1:
            return pg[j, r, 0:q_rows, :]
        first = pg[per * j, r].astype(f32)
        second = pg[per * j + 1, r].astype(f32)
        return jnp.concatenate([first, second[0:q_rows - grp * steps]], axis=0).astype(bf16)

    def one_head(i, carry):
        j = lax.rem(my_j + 1 + i, KVH)
        peaks = jnp.zeros((q_rows, TILE), f32)
        totals = jnp.zeros((q_rows, TILE), f32)
        for r in range(rows):
            q = head_rows(j, r)
            s = []
            for t in range(tiles):
                raw = lax.dot_general(q, kv[r, t, 0, j], (((1,), (1,)), ((), ())),
                                      preferred_element_type=f32) * score_scale
                s.append(jnp.where(masks[r][t], raw, very_low))
            best = s[0]
            for t in range(1, tiles):
                best = jnp.maximum(best, s[t])
            peak = jnp.max(best, axis=1, keepdims=True)
            num = jnp.zeros((q_rows, HD), f32)
            mass = jnp.zeros((q_rows, TILE), f32)
            for t in range(tiles):
                w = jnp.where(masks[r][t], jnp.exp(s[t] - peak), 0.0)
                mass = mass + w
                num = num + jnp.dot(w.astype(bf16), kv[r, t, 1, j], preferred_element_type=f32)
            total = jnp.sum(mass, axis=1, keepdims=True)
            here = lane_i == r * hq + lax.rem(row_i, hq)
            peaks = peaks + jnp.where(here, peak, 0.0)
            totals = totals + jnp.where(here, total, 0.0)
            for e in range(dests):
                pn[dests * j + e, r] = num[e * hq:(e + 1) * hq].astype(bf16)
        for e in range(dests):
            d = dests * j + e
            pk = jnp.sum(peaks[e * hq:(e + 1) * hq], axis=0, keepdims=True)
            tt = jnp.sum(totals[e * hq:(e + 1) * hq], axis=0, keepdims=True)
            sub = lax.broadcasted_iota(jnp.int32, (8, TILE), 0)
            ps[d] = jnp.where(sub == 0, pk, tt)

            @pl.when(d != me)
            def _():
                k = lax.rem(d - me + n, n)
                exchange(pn.at[d], ro_n.at[me], 2, k, d).start()
                exchange(ps.at[d], ro_s.at[me], 3, k, d).start()
        return carry

    ro_n, ro_s = ro
    lax.fori_loop(0, KVH, one_head, 0)
    ro_n[me] = pn[me]
    ro_s[me] = ps[me]

    if per == 1:
        q_own = pg[my_j, :, 0:q_rows, :].reshape(nq, HD)
        kv_own = pg[my_j, :, q_rows:q_rows + 2 * steps, :].astype(f32)
    else:
        first = pg[per * my_j].astype(f32)
        second = pg[per * my_j + 1].astype(f32)
        q_all = jnp.concatenate([first, second[:, 0:q_rows - grp * steps]], axis=1)
        part = lax.rem(me, dests)
        q_own = q_all[:, 0:hq]
        for e in range(1, dests):
            q_own = jnp.where(part == e, q_all[:, e * hq:(e + 1) * hq], q_own)
        q_own = q_own.reshape(nq, HD).astype(bf16)
        off = q_rows - grp * steps
        kv_own = second[:, off:off + 2 * steps]
    kv_own = kv_own.reshape(rows * 2 * steps, HD)
    new_k = kv_own.astype(bf16)
    new_v = pltpu.roll(kv_own, rows * 2 * steps - steps, 0).astype(bf16)
    nk = rows * 2 * steps
    qi = lax.broadcasted_iota(jnp.int32, (nq, nk), 0)
    ki = lax.broadcasted_iota(jnp.int32, (nq, nk), 1)
    q_req, k_req = qi // hq, ki // (2 * steps)
    qs, ku = qi & (steps - 1), ki & (2 * steps - 1)
    p_vec = jnp.zeros((nq, nk), jnp.int32)
    for r in range(rows):
        p_vec = jnp.where(q_req == r, pos[r], p_vec)
    valid = (q_req == k_req) & (ku <= qs) & (
        jnp.abs(((p_vec + ku) & (IMW - 1)) - ((p_vec + qs) & (IMW - 1))) <= CW)
    s_new = lax.dot_general(q_own, new_k, (((1,), (1,)), ((), ())),
                            preferred_element_type=f32) * score_scale
    top_new = jnp.max(jnp.where(valid, s_new, very_low), axis=1, keepdims=True)
    diag = (lax.broadcasted_iota(jnp.int32, (nq, TILE), 0)
            == lax.broadcasted_iota(jnp.int32, (nq, TILE), 1))
    top = jnp.sum(jnp.where(diag, top_new, 0.0), axis=0, keepdims=True)

    def column(line):
        return jnp.sum(jnp.where(diag, line, 0.0), axis=1, keepdims=True)

    for k in range(1, n):
        frm = lax.rem(me + n - k, n)
        exchange(ps.at[frm], ro_s.at[frm], 3, k, lax.rem(me + k, n)).wait_recv()
    for c in range(n):
        top = jnp.maximum(top, ro_s[c, 0:1, :])
    total = jnp.zeros((1, TILE), f32)
    factors = []
    for c in range(n):
        f = jnp.exp(ro_s[c, 0:1, :] - top)
        total = total + ro_s[c, 1:2, :] * f
        factors.append(column(f))
    w_new = jnp.where(valid, jnp.exp(s_new - column(top)), 0.0)
    total = column(total) + jnp.sum(w_new, axis=1, keepdims=True)
    numer = jnp.dot(w_new.astype(bf16), new_v, preferred_element_type=f32)
    for k in range(1, n):
        frm = lax.rem(me + n - k, n)
        exchange(pn.at[frm], ro_n.at[frm], 2, k, lax.rem(me + k, n)).wait_recv()
    for c in range(n):
        numer = numer + ro_n[c].astype(f32).reshape(nq, HD) * factors[c]
    attn = numer / total
    for r in range(rows):
        for g in range(hs):
            at = r * hq + g * steps
            arow[r * steps:(r + 1) * steps, g * HD:(g + 1) * HD] = attn[at:at + steps]
    flat = arow[...].astype(bf16)
    for c in loads_o:
        c.wait()
    po_s, po_r = po
    for k in range(1, n + 1):
        d = lax.rem(me + k, n)
        part_out = jnp.dot(flat, wo[d], preferred_element_type=f32).astype(bf16)
        if k < n:
            po_s[k] = part_out
            exchange(po_s.at[k], po_r.at[k], 4, k, d).start()
        else:
            result = part_out.astype(f32)
    for k in range(1, n):
        exchange(po_s.at[k], po_r.at[k], 4, k, lax.rem(me + k, n)).wait_recv()
        result = result + po_r[k].astype(f32)
    for r in range(rows):
        out[r] = result[r * steps:(r + 1) * steps].astype(bf16)

    for k in range(1, nb):
        batch_copy(k, b).wait_send()
    for k in range(1, n):
        d = lax.rem(me + k, n)
        exchange(xg.at[me], xg.at[me], 0, k, d).wait_send()
        exchange(pg.at[me], pg.at[me], 1, k, d).wait_send()
        exchange(pn.at[d], ro_n.at[me], 2, k, d).wait_send()
        exchange(ps.at[d], ro_s.at[me], 3, k, d).wait_send()
        exchange(po_s.at[k], po_r.at[k], 4, k, d).wait_send()


def shards(nb, n, arrivals, norm_gain, qkv_weight, out_weight, kv_cache, slot, positions,
           tile_lists):
    rows, steps, feat = arrivals.shape
    depth, cols = qkv_weight.shape
    hs = out_weight.shape[0] // HD
    hq = hs * steps
    grp = cols // HD
    smem = pl.BlockSpec(memory_space=pltpu.SMEM)
    vmem = pl.BlockSpec(memory_space=pltpu.VMEM)
    hbm = pl.BlockSpec(memory_space=pl.ANY)
    dma = pltpu.SemaphoreType.DMA
    return pl.pallas_call(
        functools.partial(kernel, nb, n),
        out_shape=jax.ShapeDtypeStruct(arrivals.shape, bf16),
        in_specs=[smem, smem, smem, vmem, vmem, hbm, hbm, hbm],
        out_specs=vmem,
        scratch_shapes=[
            pltpu.VMEM((n, feat, cols), bf16),
            pltpu.VMEM((n, out_weight.shape[0], feat), bf16),
            pltpu.VMEM(kv_cache.shape, bf16),
            pltpu.VMEM((nb * rows, steps, feat), bf16),
            pltpu.VMEM((rows * steps, feat), f32),
            pltpu.VMEM((n, rows * steps, feat), bf16),
            pltpu.VMEM((rows, grp * steps, HD), f32),
            pltpu.VMEM((n, rows, grp * steps, HD), bf16),
            pltpu.VMEM((n, rows, hq, HD), bf16),
            pltpu.VMEM((n, 8, TILE), f32),
            pltpu.VMEM((rows * steps, hs * HD), f32),
            (pltpu.VMEM((n, rows * steps, feat), bf16), pltpu.VMEM((n, rows * steps, feat), bf16)),
            (pltpu.VMEM((n, rows, hq, HD), bf16), pltpu.VMEM((n, 8, TILE), f32)),
            dma((2 * n + rows + 1,)),
            dma((5, n)),
            dma((5, n)),
            dma((nb,)),
            dma((nb,)),
        ],
        compiler_params=pltpu.CompilerParams(collective_id=0, has_side_effects=True,
                                             vmem_limit_bytes=48 << 20),
    )(slot, positions, tile_lists, arrivals, norm_gain.reshape(1, -1), qkv_weight, out_weight,
      kv_cache)


def solution(mesh):
    in_specs = (
        P("batch", None, "cache"),
        P(),
        P(None, "cache"),
        P("cache", None),
        P("batch", "cache", None, None, None, None),
        P(),
        P("batch"),
        P("batch", None),
    )
    out_specs = P("batch", None, "cache")
    body = functools.partial(shards, mesh.shape["batch"], mesh.shape["cache"])
    return jax.shard_map(body, mesh=mesh, in_specs=in_specs, out_specs=out_specs, check_vma=False)
```
